32 devices in a mesh: expert: 8 (over z, y), tensor: 4 (over x, core).
Axes of the slice: x: 2, y: 2, z: 4, core: 2. Of those that a mesh axis runs over, the one named last changes fastest.
Arguments:
- block_input: bfloat16 [8192, 2048], P('expert', 'tensor'), may hold values from -6 to 6
- cotangent: bfloat16 [8192, 2048], P('expert', 'tensor'), may hold values from -6 to 6
- lengths: int32 [8], P('expert'), may hold values from 256 to 1024, as said below
- routes: int32 [8192, 8], P('expert'), may hold values from 0 to 15, all different within a row; in each aligned block of 1024 rows (0 to 1023, 1024 to 2047, ...) at most 576 rows name the same one
- g_attn: float32 [2048], replicated, may hold values from 0.5 to 1.5
- w_query: bfloat16 [2048, 2048], P(None, 'tensor'), may hold values from -0.125 to 0.125
- w_key: bfloat16 [2048, 2048], P(None, 'tensor'), may hold values from -0.125 to 0.125
- w_value: bfloat16 [2048, 2048], P(None, 'tensor'), may hold values from -0.125 to 0.125
- g_query: float32 [2048], P('tensor'), may hold values from 0.5 to 1.5
- g_key: float32 [2048], P('tensor'), may hold values from 0.5 to 1.5
- w_out: bfloat16 [2048, 2048], P('tensor'), may hold values from -0.5 to 0.5
- g_moe: float32 [2048], replicated, may hold values from 0.5 to 1.5
- w_router: bfloat16 [2048, 16], replicated, may hold values from -0.125 to 0.125
- w_gate: bfloat16 [16, 2048, 1024], P('expert', None, 'tensor'), may hold values from -0.125 to 0.125
- w_up: bfloat16 [16, 2048, 1024], P('expert', None, 'tensor'), may hold values from -0.125 to 0.125
- w_down: bfloat16 [16, 1024, 2048], P('expert', 'tensor'), may hold values from -6 to 6
Outputs:
- output: bfloat16 [8192, 2048], P('expert', 'tensor')
- grad_input: bfloat16 [8192, 2048], P('expert', 'tensor')
- grad_g_attn: float32 [2048], replicated
- grad_w_query: float32 [2048, 2048], P(None, 'tensor')
- grad_w_key: float32 [2048, 2048], P(None, 'tensor')
- grad_w_value: float32 [2048, 2048], P(None, 'tensor')
- grad_g_query: float32 [2048], P('tensor')
- grad_g_key: float32 [2048], P('tensor')
- grad_w_out: float32 [2048, 2048], P('tensor')
- grad_g_moe: float32 [2048], replicated
- grad_w_router: float32 [2048, 16], replicated
- grad_w_gate: float32 [16, 2048, 1024], P('expert', None, 'tensor')
- grad_w_up: float32 [16, 2048, 1024], P('expert', None, 'tensor')
- grad_w_down: float32 [16, 1024, 2048], P('expert', 'tensor')
The draws below stay inside these ranges and needn't reach their ends.
Inputs may be any that keep to these rules, and one draw needn't show every extreme that they name: `lengths`: some slot has length 1024 and some has length 256. `routes`: the 8 experts of a token differ; among the rows of one device (aligned blocks of 1024 rows) no expert is named more than 576 times, a bound that some block reaches.
All inputs are finite; a program needn't handle non-finite values.
Results may differ from the reference program's by a relative error of at most 0.028.
Values may be sent and summed in bfloat16 or wider, within the bound.
No kernel may reach another device: no remote copies, remote signals or barrier semaphores. Data moves between devices by JAX's collectives and lax.ppermute only.
A program may use at most 576 MiB of HBM per device.

```python
import math
import jax
import jax.numpy as jnp
import numpy as np
from jax import lax

D = 2048
H = 16
HD = 128
FF = 1024
TOPK = 8
SLOT = 1024
MINLEN = 256
E = 16
TOK_DEV = 1024
TOKENS = 8192
SLOTS = 8
CAP = 576
N_EXPERT = 8


def draw_lengths(key, part):
    base = jax.random.fold_in(key, 7101)
    first_key, second_key, third_key = jax.random.split(base, 3)
    lengths = jax.random.randint(first_key, (SLOTS,), MINLEN, SLOT + 1)
    full_at = jax.random.randint(second_key, (), 0, SLOTS)
    lengths = lengths.at[full_at].set(SLOT)
    least_at = (full_at + 1 + jax.random.randint(third_key, (), 0, SLOTS - 1)) % SLOTS
    return lengths.at[least_at].set(MINLEN).astype(jnp.int32)


def level_of(own_key, extent, shards, low, largest):
    gain = 1.0
    for axis_at, blocks in shards:
        heights = jax.random.uniform(jax.random.fold_in(jax.random.fold_in(own_key, 6), axis_at), (blocks,), jnp.float32, low / len(shards), largest / len(shards))
        gain = gain * jnp.repeat(jnp.exp(heights), extent[axis_at] // blocks).reshape((-1,) + (1,) * (len(extent) - 1 - axis_at))
    return gain


def shared_out(own_key, own, number, rows, amount, top, bound, slope):
    order = jax.random.permutation(own_key, amount)
    packed, usual = shares(amount, rows * top, bound, slope, True), shares(amount, rows * top, bound, slope, False)
    places = jnp.arange(amount)

    def named(tallies, turn):
        used = int((tallies > 0).sum())
        fixed = max(1, used // 4)
        shifted = fixed + (places - fixed + turn * (used - fixed)) % max(1, amount - fixed)
        return jnp.zeros((amount,), jnp.int32).at[order[jnp.where(places < fixed, places, shifted)]].set(jnp.asarray(tallies, jnp.int32))

    tallies = jnp.where(number % 4 == 0, named(packed, number // 4), named(usual, number - number // 4 - 1))
    mixed = jax.random.permutation(jax.random.fold_in(own, 3), amount)
    donor, sink = mixed[0:amount // 2 * 2:2], mixed[1:amount // 2 * 2:2]
    slack = jnp.minimum(tallies[donor] - 1, bound - tallies[sink]) // 2
    slack = jnp.where((donor == order[0]) | (sink == order[0]) | (tallies[sink] == 0), 0, jnp.maximum(slack, 0))
    shifted = jax.random.randint(jax.random.fold_in(own, 4), (amount // 2,), 0, 1 << 20) % (slack + 1)
    tallies = tallies.at[donor].add(-shifted).at[sink].add(shifted)
    items = jnp.searchsorted(jnp.cumsum(tallies), jnp.arange(rows * top), side="right").astype(jnp.int32)
    listing = items.reshape(top, rows).T
    listing = listing[jax.random.permutation(jax.random.fold_in(own, 1), rows)]
    turn = jax.random.randint(jax.random.fold_in(own, 2), (rows, 1), 0, top)
    return jnp.take_along_axis(listing, (jnp.arange(top)[None, :] + turn) % top, axis=1)


def shares(number_of, total, bound, skew, full):
    weights = [(1 << 20) // math.isqrt(standing ** skew) + 1 for standing in range(1, number_of + 1)]
    largest = bound if full else min(bound, max(-(-total // number_of), total * weights[0] // sum(weights)))
    least = 1 if total - largest >= number_of - 1 else 0
    given, spare = [largest] + [least] * (number_of - 1), total - largest - least * (number_of - 1)
    while spare > 0:
        free = [i for i in range(1, number_of) if given[i] < largest] or [i for i in range(1, number_of) if given[i] < bound]
        whole, remaining = sum([weights[i] for i in free]), spare
        for i in free:
            addition = min(bound - given[i], max(1, remaining * weights[i] // whole), spare)
            given[i] = given[i] + addition
            spare = spare - addition
    return np.array(given)


def normal_values(stream_key, dims, spread, limit, shards=(), held_as=jnp.bfloat16):
    values = jax.random.normal(stream_key, dims, jnp.float32) * spread
    if len(shards) > 0:
        values = level_of(stream_key, dims, shards, -0.22, 0.18) * values
    return jnp.clip(values, min=-limit, max=limit).astype(held_as)


def setup_inputs(seed: int = 0) -> dict:
    streams_of = jax.random.split(jax.random.key(seed), 17)
    block_input = normal_values(streams_of[0], (TOKENS, D), 1.0, 6.0, ((0, 8), (1, 4)))
    cotangent = normal_values(streams_of[1], (TOKENS, D), 1.0, 6.0, ((0, 8), (1, 4)))
    lengths = draw_lengths(jax.random.fold_in(streams_of[16], 71), 0)
    routes_keys = jax.random.split(jax.random.fold_in(streams_of[3], 1), TOKENS // TOK_DEV)
    routes_turns = jax.random.permutation(jax.random.fold_in(streams_of[3], 3), TOKENS // TOK_DEV)
    routes = jax.vmap(lambda own, number: shared_out(jax.random.fold_in(streams_of[3], 2), own, number, TOK_DEV, E, TOPK, CAP, 2))(routes_keys, routes_turns).reshape((TOKENS, TOPK))
    g_attn = jnp.clip(1.0 + 0.1 * jax.random.normal(streams_of[4], (D,), jnp.float32), 0.5, 1.5)
    w_query = normal_values(streams_of[5], (D, D), D ** -0.5, 0.125, ((1, 4),))
    w_key = normal_values(streams_of[6], (D, D), D ** -0.5, 0.125, ((1, 4),))
    w_value = normal_values(streams_of[7], (D, D), D ** -0.5, 0.125, ((1, 4),))
    g_query = jnp.clip(1.0 + 0.1 * jax.random.normal(streams_of[8], (D,), jnp.float32), 0.5, 1.5)
    g_key = jnp.clip(1.0 + 0.1 * jax.random.normal(streams_of[9], (D,), jnp.float32), 0.5, 1.5)
    w_out = normal_values(streams_of[10], (D, D), (D // 16) ** -0.5, 0.5, ((0, 4),))
    g_moe = jnp.clip(1.0 + 0.1 * jax.random.normal(streams_of[11], (D,), jnp.float32), 0.5, 1.5)
    w_router = normal_values(streams_of[12], (D, E), D ** -0.5, 0.125)
    w_gate = normal_values(streams_of[13], (E, D, FF), D ** -0.5, 0.125, ((0, 8), (2, 4)))
    w_up = normal_values(streams_of[14], (E, D, FF), D ** -0.5, 0.125, ((0, 8), (2, 4)))
    w_down = normal_values(streams_of[15], (E, FF, D), 1 ** -0.5, 6.0, ((0, 8), (1, 4)))
    return {"block_input": block_input, "cotangent": cotangent, "lengths": lengths, "routes": routes, "g_attn": g_attn, "w_query": w_query, "w_key": w_key, "w_value": w_value, "g_query": g_query, "g_key": g_key, "w_out": w_out, "g_moe": g_moe, "w_router": w_router, "w_gate": w_gate, "w_up": w_up, "w_down": w_down}


EPS = 1e-05
THETA = 10000.0
HIGH = lax.Precision.HIGHEST

@jax.custom_vjp
def low(v):
    return lax.optimization_barrier(v.astype(jnp.bfloat16)).astype(jnp.float32)

@jax.custom_vjp
def low_back(v):
    return v

def low_keep(v):
    return (low(v), None)

def low_pass(kept, grad):
    return (grad,)

def back_keep(v):
    return (v, None)

def back_low(kept, grad):
    return (low(grad),)
low.defvjp(low_keep, low_pass)
low_back.defvjp(back_keep, back_low)

def dense(operand, matrix):
    return jnp.dot(operand, matrix, precision=HIGH, preferred_element_type=jnp.float32)

def norm_scale(values):
    return lax.rsqrt(lax.optimization_barrier(jnp.mean(values * values, axis=-1, keepdims=True)) + EPS)

def rotary_tables():
    frequency = THETA ** (-jnp.arange(0, HD // 2, dtype=jnp.float32) * 2.0 / HD)
    angles = jnp.arange(SLOT, dtype=jnp.float32)[:, None] * frequency[None, :]
    return (jnp.cos(angles)[:, None, :], jnp.sin(angles)[:, None, :])

def rotate(values, cosine, sine_table):
    half_size = values.shape[-1] // 2
    first_half = values[..., :half_size]
    second = values[..., half_size:]
    return jnp.concatenate([first_half * cosine - second * sine_table, second * cosine + first_half * sine_table], axis=-1)

def attend(inputs):
    query_heads, key_heads, value_heads, length = inputs
    raw_scores = jnp.einsum('qhd,khd->hqk', query_heads, key_heads, precision=HIGH)
    scores = low_back(raw_scores) * HD ** (-0.5)
    positions = jnp.arange(SLOT)
    allowed = (positions[None, :] <= positions[:, None]) & (positions[None, :] < length)
    scores = jnp.where(allowed[None], scores, -1e+30)
    weights = low(jax.nn.softmax(scores, axis=-1))
    return jnp.einsum('hqk,khd->qhd', weights, value_heads, precision=HIGH)

def forward(lengths, routes, block_input, g_attn, w_query, w_key, w_value, g_query, g_key, w_out, g_moe, w_router, w_gate, w_up, w_down):
    positions = jnp.arange(TOKENS) % SLOT
    live_rows = positions < jnp.repeat(lengths, SLOT, total_repeat_length=TOKENS)
    valid_rows = live_rows.astype(jnp.float32)[:, None]
    normed = low(block_input * norm_scale(block_input) * g_attn)
    q_raw = low_back(dense(normed, w_query))
    k_raw = low_back(dense(normed, w_key))
    values = low_back(low(dense(normed, w_value)))
    q_norm = q_raw * norm_scale(q_raw) * g_query
    k_norm = k_raw * norm_scale(k_raw) * g_key
    cosine, sine_table = rotary_tables()
    head_shape = (SLOTS, SLOT, H, HD)
    query_heads = low(rotate(q_norm.reshape(head_shape), cosine, sine_table))
    key_heads = low(rotate(k_norm.reshape(head_shape), cosine, sine_table))
    mixed = lax.map(jax.checkpoint(attend), (query_heads, key_heads, values.reshape(head_shape), lengths))
    heads_out = low_back(low(mixed.reshape(TOKENS, D)))
    hidden = block_input + low_back(dense(heads_out, w_out))
    moe_in = low(hidden * norm_scale(hidden) * g_moe)
    logits = low_back(dense(moe_in, w_router))
    router_probs = jax.nn.softmax(logits, axis=-1)
    chosen = (routes[:, :, None] == jnp.arange(E, dtype=jnp.int32)[None, None, :]).astype(jnp.float32)
    gates = jnp.einsum('te,tje->tj', router_probs, chosen, precision=HIGH) * valid_rows
    flat_routes = routes.reshape(TOKENS * TOPK)
    pair_live = jnp.repeat(live_rows, TOPK, total_repeat_length=TOKENS * TOPK)
    in_padded = jnp.concatenate([moe_in, jnp.zeros((1, D), jnp.float32)], axis=0)
    gate_padded = jnp.concatenate([gates.reshape(TOKENS * TOPK), jnp.zeros((1,), jnp.float32)])

    def expert_step(carry, inputs):
        expert, gate_weight, up_weight, down_weight = inputs
        picked = jnp.nonzero((flat_routes == expert) & pair_live, size=N_EXPERT * CAP, fill_value=TOKENS * TOPK)[0]
        token_index = picked // TOPK
        expert_rows = low_back(in_padded[token_index])
        gate_pre = low_back(dense(expert_rows, gate_weight))
        up_pre = low_back(dense(expert_rows, up_weight))
        inner = low(jax.nn.silu(gate_pre) * up_pre)
        result = low_back(low(dense(inner, down_weight)))
        return (carry.at[token_index].add(result * gate_padded[picked][:, None]), None)
    moe_total, unused = lax.scan(jax.checkpoint(expert_step), jnp.zeros((TOKENS + 1, D), jnp.float32), (jnp.arange(E, dtype=jnp.int32), w_gate, w_up, w_down))
    return valid_rows * (hidden + moe_total[:TOKENS])

def reference(block_input, cotangent, lengths, routes, g_attn, w_query, w_key, w_value, g_query, g_key, w_out, g_moe, w_router, w_gate, w_up, w_down):
    floats = [entry.astype(jnp.float32) for entry in (block_input, g_attn, w_query, w_key, w_value, g_query, g_key, w_out, g_moe, w_router, w_gate, w_up, w_down)]

    def run(*params):
        return forward(lengths, routes, *params)
    output, pullback = jax.vjp(run, *floats)
    grads = pullback(cotangent.astype(jnp.float32))
    return (output.astype(jnp.bfloat16), grads[0].astype(jnp.bfloat16), grads[1], grads[2], grads[3], grads[4], grads[5], grads[6], grads[7], grads[8], grads[9], grads[10], grads[11], grads[12])
```

```python
import functools

import jax
import jax.numpy as jnp
from jax import lax
from jax.experimental import pallas as pl
from jax.experimental.pallas import tpu as pltpu
from jax.sharding import PartitionSpec as P

HD = 128
TOPK = 8
SLOT = 1024


EPS = 1e-05
THETA = 10000.0
NEGATIVE = -1e30


def cross_dot(operand, other_side):
    return lax.dot_general(
        operand, other_side, (((0,), (0,)), ((), ())), preferred_element_type=jnp.float32
    )


def dot_transposed(operand, other_side):
    return lax.dot_general(
        operand, other_side, (((1,), (1,)), ((), ())), preferred_element_type=jnp.float32
    )


def rotary_tables(length, head_size):
    frequency = THETA ** (-jnp.arange(0, head_size // 2, dtype=jnp.float32) * 2.0 / head_size)
    angles = jnp.arange(length, dtype=jnp.float32)[:, None] * frequency[None, :]
    return (jnp.cos(angles)[:, None, :], jnp.sin(angles)[:, None, :])


def rotate(values, cosine, sine_table):
    half_size = values.shape[-1] // 2
    first_half = values[..., :half_size]
    second = values[..., half_size:]
    return jnp.concatenate(
        [first_half * cosine - second * sine_table, second * cosine + first_half * sine_table],
        axis=-1,
    )


def unrotate(gradient, cosine, sine_table):
    half_size = gradient.shape[-1] // 2
    first_half = gradient[..., :half_size]
    second = gradient[..., half_size:]
    return jnp.concatenate(
        [first_half * cosine + second * sine_table, second * cosine - first_half * sine_table],
        axis=-1,
    )


def block_scores(query_block, key_prefix, block_start, length, factor):
    raw_scores = jnp.einsum(
        "qhd,khd->hqk", query_block, key_prefix, preferred_element_type=jnp.float32
    )
    query_pos = block_start + jnp.arange(query_block.shape[0])
    key_pos = jnp.arange(key_prefix.shape[0])
    allowed = (key_pos[None, :] <= query_pos[:, None]) & (key_pos[None, :] < length)
    return (raw_scores * factor, allowed[None])


def moe_body(
    resume,
    starts,
    lens,
    x_ref,
    g_ref,
    info_ref,
    wgu_ref,
    wd_ref,
    gate_before,
    up_before,
    down_before,
    out_ref,
    dx_ref,
    dgate_ref,
    gate_grad,
    up_grad,
    down_grad,
    acc_in,
    acc_down,
    sem,
):
    n_local, width = gate_grad.shape[0], gate_grad.shape[2]
    hidden = n_local * width
    pieces, rows, cols = x_ref.shape
    slot, block = pl.program_id(0), pl.program_id(1)

    def move(gate_hbm, up_hbm, down_hbm, store):
        pairs = []
        for e in range(n_local):
            at = pl.ds(e * width, width)
            pairs.append((acc_in.at[:, at], gate_hbm.at[e]))
            pairs.append((acc_in.at[:, pl.ds(hidden + e * width, width)], up_hbm.at[e]))
            pairs.append((acc_down.at[at, :], down_hbm.at[e]))
        started = []
        for k, (inside, outside) in enumerate(pairs):
            ends = (inside, outside) if store else (outside, inside)
            copy = pltpu.make_async_copy(*ends, sem.at[k])
            copy.start()
            started.append(copy)
        for copy in started:
            copy.wait()

    @pl.when((slot == 0) & (block == 0))
    def _():
        if resume:
            move(gate_before, up_before, down_before, False)
        else:
            acc_in[...] = jnp.zeros_like(acc_in)
            acc_down[...] = jnp.zeros_like(acc_down)

    live = starts[0] + block * rows < lens[slot]

    @pl.when(live)
    def _():
        scale = info_ref[:, n_local : n_local + 1]
        pre = jnp.zeros((rows, 2 * hidden), jnp.float32)
        d_raw = jnp.zeros((rows, hidden), jnp.float32)
        for p in range(pieces):
            span = slice(p * cols, (p + 1) * cols)
            pre += jnp.dot(x_ref[p], wgu_ref[span, :], preferred_element_type=jnp.float32)
            d_raw += dot_transposed(g_ref[p], wd_ref[:, span])
        inner_parts, gate_parts, up_parts = [], [], []
        for e in range(n_local):
            at = slice(e * width, (e + 1) * width)
            gate_pre = pre[:, at] * scale
            up_pre = pre[:, hidden + e * width : hidden + (e + 1) * width] * scale
            gate = info_ref[:, e : e + 1]
            sigma = jax.nn.sigmoid(gate_pre)
            silu_value = gate_pre * sigma
            inner = silu_value * up_pre
            raw = d_raw[:, at]
            dgate_ref[:, e : e + 1] = jnp.sum(inner * raw, axis=1, keepdims=True)
            d_inner = raw * (gate * scale)
            inner_parts.append((inner * gate).astype(jnp.bfloat16))
            gate_parts.append(
                (d_inner * up_pre * sigma * (1.0 + gate_pre * (1.0 - sigma))).astype(jnp.bfloat16)
            )
            up_parts.append((d_inner * silu_value).astype(jnp.bfloat16))
        inner_all = jnp.concatenate(inner_parts, axis=1)
        d_pre = jnp.concatenate(gate_parts + up_parts, axis=1)
        for p in range(pieces):
            span = slice(p * cols, (p + 1) * cols)
            out_ref[p] = jnp.dot(
                inner_all, wd_ref[:, span], preferred_element_type=jnp.float32
            ).astype(jnp.bfloat16)
            dx_ref[p] = dot_transposed(d_pre, wgu_ref[span, :]).astype(jnp.bfloat16)
            acc_in[span, :] += cross_dot(x_ref[p], d_pre)
            acc_down[:, span] += cross_dot(inner_all, g_ref[p])

    @pl.when(jnp.logical_not(live))
    def _():
        out_ref[...] = jnp.zeros_like(out_ref)
        dx_ref[...] = jnp.zeros_like(dx_ref)
        dgate_ref[...] = jnp.zeros_like(dgate_ref)

    @pl.when((slot == pl.num_programs(0) - 1) & (block == pl.num_programs(1) - 1))
    def _():
        move(gate_grad, up_grad, down_grad, True)


def moe_call(start, lens, x_all, g_all, info, wgu, wd, n_local, before):
    slots, pieces, rows, cols = x_all.shape
    width = wd.shape[0] // n_local
    model = pieces * cols
    tile = min(256, rows)

    def row_block(minor):
        return pl.BlockSpec((None, tile, minor), lambda s, b, *_: (s, b, 0))

    def piece_block():
        return pl.BlockSpec((None, pieces, tile, cols), lambda s, b, *_: (s, 0, b, 0))

    def whole(shape):
        return pl.BlockSpec(shape, lambda s, b, *_: (0, 0), pipeline_mode=pl.Buffered(1))

    f32 = jnp.float32
    anywhere = pl.BlockSpec(memory_space=pl.ANY)
    resume = before is not None
    if not resume:
        before = [jnp.zeros((8, 128), f32)] * 3
    return pl.pallas_call(
        functools.partial(moe_body, resume),
        out_shape=(
            jax.ShapeDtypeStruct(x_all.shape, jnp.bfloat16),
            jax.ShapeDtypeStruct(x_all.shape, jnp.bfloat16),
            jax.ShapeDtypeStruct(info.shape, f32),
            jax.ShapeDtypeStruct((n_local, model, width), f32),
            jax.ShapeDtypeStruct((n_local, model, width), f32),
            jax.ShapeDtypeStruct((n_local, width, model), f32),
        ),
        grid_spec=pltpu.PrefetchScalarGridSpec(
            num_scalar_prefetch=2,
            grid=(slots, rows // tile),
            in_specs=[
                piece_block(),
                piece_block(),
                row_block(info.shape[2]),
                whole(wgu.shape),
                whole(wd.shape),
                anywhere,
                anywhere,
                anywhere,
            ],
            out_specs=[
                piece_block(),
                piece_block(),
                row_block(info.shape[2]),
                anywhere,
                anywhere,
                anywhere,
            ],
            scratch_shapes=[
                pltpu.VMEM((model, wgu.shape[1]), f32),
                pltpu.VMEM(wd.shape, f32),
                pltpu.SemaphoreType.DMA((3 * n_local,)),
            ],
        ),
        input_output_aliases={7: 3, 8: 4, 9: 5} if resume else {},
        name="experts",
    )(start, lens, x_all, g_all, info, wgu, wd, *before)


def shards(
    block_input,
    cotangent,
    lengths,
    routes,
    g_attn,
    w_query,
    w_key,
    w_value,
    g_query,
    g_key,
    w_out,
    g_moe,
    w_router,
    w_gate,
    w_up,
    w_down,
):
    tok_rows, slice_width = block_input.shape
    n_tensor = lax.axis_size("tensor")
    n_expert = lax.axis_size("expert")
    everyone = ("expert", "tensor")
    model_width = slice_width * n_tensor
    n_experts = w_router.shape[1]
    n_local = w_gate.shape[0]
    heads_here = w_query.shape[1] // HD
    factor = HD ** (-0.5)
    e_index = lax.axis_index("expert")
    offset = lax.axis_index("tensor") * slice_width
    block_rows = min(512, SLOT)
    n_chunks = max(1, n_expert // 4) if n_expert > 8 else 1
    chunk_rows = tok_rows // n_chunks

    def own_columns(vector):
        return lax.dynamic_slice_in_dim(vector, offset, slice_width, vector.ndim - 1)

    full_input = lax.all_gather(block_input, "tensor", axis=1, tiled=True)
    early, _ = lax.optimization_barrier((cotangent, full_input))
    all_lengths = lax.all_gather(lengths, "expert", axis=0, tiled=True)
    positions = jnp.arange(tok_rows)
    live_rows = positions < lengths[0]
    valid_rows = live_rows.astype(jnp.float32)[:, None]
    input_full = full_input.astype(jnp.float32)
    scale_x = lax.rsqrt(jnp.mean(input_full * input_full, axis=-1, keepdims=True) + EPS)
    normed = (input_full * scale_x * g_attn).astype(jnp.bfloat16)
    q_raw = jnp.dot(normed, w_query, preferred_element_type=jnp.float32)
    k_raw = jnp.dot(normed, w_key, preferred_element_type=jnp.float32)
    values = jnp.dot(normed, w_value, preferred_element_type=jnp.float32).astype(jnp.bfloat16)
    q_total, k_total = lax.psum(
        (jnp.sum(q_raw * q_raw, axis=1), jnp.sum(k_raw * k_raw, axis=1)), "tensor"
    )
    scale_q = lax.rsqrt(q_total / model_width + EPS)[:, None]
    scale_k = lax.rsqrt(k_total / model_width + EPS)[:, None]
    q_norm = q_raw * scale_q * g_query
    k_norm = k_raw * scale_k * g_key
    cosine, sine_table = rotary_tables(SLOT, HD)
    head_shape = (SLOT, heads_here, HD)
    query_heads = rotate(q_norm.reshape(head_shape), cosine, sine_table).astype(jnp.bfloat16)
    key_heads = rotate(k_norm.reshape(head_shape), cosine, sine_table).astype(jnp.bfloat16)
    value_heads = values.reshape(head_shape)
    outputs = []
    log_totals = []
    for block_start in range(0, SLOT, block_rows):
        block_end = block_start + block_rows
        scores, allowed = block_scores(
            query_heads[block_start:block_end], key_heads[:block_end], block_start, lengths[0], factor
        )
        masked = jnp.where(allowed, scores, NEGATIVE)
        row_max = jnp.max(masked, axis=-1, keepdims=True)
        exponent_terms = jnp.exp(masked - row_max)
        row_total = jnp.sum(exponent_terms, axis=-1, keepdims=True)
        weights = (exponent_terms / row_total).astype(jnp.bfloat16)
        outputs.append(
            jnp.einsum(
                "hqk,khd->qhd", weights, value_heads[:block_end], preferred_element_type=jnp.float32
            )
        )
        log_totals.append(row_max + jnp.log(row_total))
    heads_out = (
        jnp.concatenate(outputs, axis=0).reshape(tok_rows, heads_here * HD).astype(jnp.bfloat16)
    )
    attn_part = jnp.dot(heads_out, w_out, preferred_element_type=jnp.float32).astype(jnp.bfloat16)
    attn_slice = lax.psum_scatter(attn_part, "tensor", scatter_dimension=1, tiled=True)
    hidden = block_input.astype(jnp.float32) + attn_slice.astype(jnp.float32)
    g_moe_slice = own_columns(g_moe)
    moe_rows = (hidden * g_moe_slice).astype(jnp.bfloat16)
    router_slice = lax.dynamic_slice_in_dim(w_router, offset, slice_width, 0)
    statistics = jnp.concatenate(
        [
            jnp.dot(moe_rows, router_slice, preferred_element_type=jnp.float32),
            jnp.sum(hidden * hidden, axis=1, keepdims=True),
        ],
        axis=1,
    )
    statistics = lax.psum(statistics, "tensor")
    scale_h = lax.rsqrt(statistics[:, n_experts:] / model_width + EPS)
    router_probs = jax.nn.softmax(statistics[:, :n_experts] * scale_h, axis=-1)
    expert_ids = jnp.arange(n_experts, dtype=jnp.int32)
    chosen = jnp.any(routes[:, :, None] == expert_ids[None, None, :], axis=1) & live_rows[:, None]
    chosen = chosen.astype(jnp.float32)
    gates = router_probs * chosen
    info = lax.all_gather(jnp.concatenate([gates, scale_h], axis=1).T, "expert", axis=0)
    info = jnp.concatenate(
        [
            lax.dynamic_slice_in_dim(info, e_index * n_local, n_local, 1),
            info[:, n_experts:],
            jnp.zeros((n_expert, 8 - n_local - 1, tok_rows), jnp.float32),
        ],
        axis=1,
    ).transpose(0, 2, 1)
    wgu = jnp.concatenate([w_gate[e] for e in range(n_local)] + [w_up[e] for e in range(n_local)], axis=1)
    wd = w_down.reshape(-1, model_width)

    moe_parts, back_parts, dgate_parts, own_rows, own_dy = [], [], [], [], []
    weight_grads = None
    chain = None
    for chunk in range(n_chunks):
        at = slice(chunk * chunk_rows, (chunk + 1) * chunk_rows)
        x_piece, g_piece = moe_rows[at], early[at]
        if chain is not None:
            x_piece, g_piece, chain = lax.optimization_barrier((x_piece, g_piece, chain))
            back_parts[-1], moe_parts[-1], own_rows[-1], own_dy[-1], weight_grads = chain
        shape = (n_expert, n_tensor, chunk_rows, slice_width)
        g_all = lax.all_gather(g_piece, everyone, axis=0).reshape(shape)
        x_all = lax.all_gather(x_piece, everyone, axis=0).reshape(shape)
        own_rows.append(lax.dynamic_index_in_dim(x_all, e_index, 0, False))
        own_dy.append(lax.dynamic_index_in_dim(g_all, e_index, 0, False))
        out_part, dx_part, dgate, *weight_grads = moe_call(
            jnp.full((1,), chunk * chunk_rows, jnp.int32),
            all_lengths,
            x_all,
            g_all,
            info[:, at],
            wgu,
            wd,
            n_local,
            weight_grads,
        )
        flat = (n_expert * n_tensor, chunk_rows, slice_width)
        back_parts.append(lax.psum_scatter(dx_part.reshape(flat), everyone, scatter_dimension=0))
        moe_parts.append(lax.psum_scatter(out_part.reshape(flat), everyone, scatter_dimension=0))
        dgate_parts.append(dgate)
        chain = (back_parts[-1], moe_parts[-1], own_rows[-1], own_dy[-1], weight_grads)
    grad_w_gate, grad_w_up, grad_w_down = weight_grads
    moe_slice = jnp.concatenate(moe_parts, axis=0).astype(jnp.float32)
    back_slice = jnp.concatenate(back_parts, axis=0).astype(jnp.float32)
    output = (valid_rows * (hidden + moe_slice)).astype(jnp.bfloat16)

    def side_by_side(parts):
        rows = jnp.concatenate(parts, axis=1)
        return rows.transpose(1, 0, 2).reshape(tok_rows, model_width)

    rows_full = side_by_side(own_rows).astype(jnp.float32)
    d_out_full = side_by_side(own_dy).astype(jnp.float32) * valid_rows
    d_gates = jnp.concatenate(dgate_parts, axis=1)[:, :, :n_local].transpose(0, 2, 1)
    d_gates = lax.all_to_all(d_gates, "expert", split_axis=0, concat_axis=0, tiled=True)
    d_gates = lax.psum(d_gates.reshape(n_experts, tok_rows), "tensor").T
    d_probs = d_gates * chosen
    d_logits = (
        router_probs * (d_probs - jnp.sum(router_probs * d_probs, axis=-1, keepdims=True))
    ).astype(jnp.bfloat16)
    scaled_logits = (d_logits.astype(jnp.float32) * scale_h).astype(jnp.bfloat16)
    router_grad = cross_dot(moe_rows, scaled_logits)
    back_slice = back_slice + dot_transposed(scaled_logits, router_slice)
    back_full = lax.all_gather(back_slice.astype(jnp.bfloat16), "tensor", axis=1, tiled=True)
    back_full = back_full.astype(jnp.float32)
    projection = jnp.mean(back_full * rows_full, axis=-1, keepdims=True) * scale_h
    h_term = projection * scale_h
    d_hidden = d_out_full + g_moe * back_full - rows_full / g_moe * h_term
    d_attn = d_hidden.astype(jnp.bfloat16)
    d_out_slice = cotangent.astype(jnp.float32) * valid_rows
    d_hidden_slice = d_out_slice + g_moe_slice * back_slice - hidden * h_term
    grad_g_moe = jnp.sum(back_slice * hidden, axis=0)
    grad_w_out = cross_dot(heads_out, d_attn)
    d_heads = dot_transposed(d_attn, w_out).astype(jnp.bfloat16).reshape(head_shape)
    d_query_parts = []
    block_number = 0
    d_keys = jnp.zeros((SLOT, heads_here, HD), jnp.float32)
    d_value_sum = jnp.zeros((SLOT, heads_here, HD), jnp.float32)
    for block_start in range(0, SLOT, block_rows):
        block_end = block_start + block_rows
        query_block = query_heads[block_start:block_end]
        key_prefix = key_heads[:block_end]
        value_prefix = value_heads[:block_end]
        scores, allowed = block_scores(query_block, key_prefix, block_start, lengths[0], factor)
        probs = jnp.where(allowed, jnp.exp(scores - log_totals[block_number]), 0.0)
        block_number += 1
        d_block = d_heads[block_start:block_end]
        d_probs_att = jnp.einsum(
            "qhd,khd->hqk", d_block, value_prefix, preferred_element_type=jnp.float32
        )
        spread = jnp.sum(probs * d_probs_att, axis=-1, keepdims=True)
        d_scores = (factor * probs * (d_probs_att - spread)).astype(jnp.bfloat16)
        d_query_parts.append(
            jnp.einsum("hqk,khd->qhd", d_scores, key_prefix, preferred_element_type=jnp.float32)
        )
        d_keys = d_keys.at[:block_end].add(
            jnp.einsum("hqk,qhd->khd", d_scores, query_block, preferred_element_type=jnp.float32)
        )
        d_value_sum = d_value_sum.at[:block_end].add(
            jnp.einsum(
                "hqk,qhd->khd", probs.astype(jnp.bfloat16), d_block, preferred_element_type=jnp.float32
            )
        )
    d_query = jnp.concatenate(d_query_parts, axis=0)
    d_values = d_value_sum.reshape(tok_rows, heads_here * HD).astype(jnp.bfloat16)
    d_q_norm = unrotate(d_query, cosine, sine_table).reshape(tok_rows, heads_here * HD)
    d_k_norm = unrotate(d_keys, cosine, sine_table).reshape(tok_rows, heads_here * HD)
    q_sum, k_sum = lax.psum(
        (jnp.sum(d_q_norm * g_query * q_raw, axis=1), jnp.sum(d_k_norm * g_key * k_raw, axis=1)),
        "tensor",
    )
    grad_g_query = jnp.sum(d_q_norm * q_raw * scale_q, axis=0)
    grad_g_key = jnp.sum(d_k_norm * k_raw * scale_k, axis=0)
    d_q_raw = (
        scale_q * g_query * d_q_norm - q_raw * scale_q**3 * (q_sum / model_width)[:, None]
    ).astype(jnp.bfloat16)
    d_k_raw = (
        scale_k * g_key * d_k_norm - k_raw * scale_k**3 * (k_sum / model_width)[:, None]
    ).astype(jnp.bfloat16)
    grad_w_query = cross_dot(normed, d_q_raw)
    grad_w_key = cross_dot(normed, d_k_raw)
    grad_w_value = cross_dot(normed, d_values)
    d_normed_part = (
        dot_transposed(d_q_raw, w_query)
        + dot_transposed(d_k_raw, w_key)
        + dot_transposed(d_values, w_value)
    )
    column_sums = jnp.sum(
        d_q_raw.astype(jnp.float32) * q_raw
        + d_k_raw.astype(jnp.float32) * k_raw
        + d_values.astype(jnp.float32) * values.astype(jnp.float32),
        axis=1,
    )
    x_mean = (lax.psum(column_sums, "tensor") / model_width)[:, None]
    d_normed = lax.psum_scatter(
        d_normed_part.astype(jnp.bfloat16), "tensor", scatter_dimension=1, tiled=True
    ).astype(jnp.float32)
    x_hat = block_input.astype(jnp.float32) * scale_x
    grad_g_attn = jnp.sum(d_normed * x_hat, axis=0)
    grad_input = (
        d_hidden_slice + scale_x * (d_normed * own_columns(g_attn) - x_hat * x_mean)
    ).astype(jnp.bfloat16)

    def summed(grad):
        return lax.psum(grad.astype(jnp.bfloat16), "expert").astype(jnp.float32)

    small = jnp.concatenate(
        [router_grad.T, grad_g_moe[None], grad_g_attn[None], grad_g_query[None], grad_g_key[None]],
        axis=0,
    )
    small = lax.psum(small, "expert")
    shared = lax.all_gather(small[: n_experts + 2], "tensor", axis=1, tiled=True)
    return (
        output,
        grad_input,
        shared[n_experts + 1],
        summed(grad_w_query),
        summed(grad_w_key),
        summed(grad_w_value),
        small[n_experts + 2],
        small[n_experts + 3],
        summed(grad_w_out),
        shared[n_experts],
        shared[:n_experts].T,
        grad_w_gate,
        grad_w_up,
        grad_w_down,
    )


def solution(mesh):
    placed = (
        P("expert", "tensor"),
        P("expert", "tensor"),
        P("expert"),
        P("expert", None),
        P(),
        P(None, "tensor"),
        P(None, "tensor"),
        P(None, "tensor"),
        P("tensor"),
        P("tensor"),
        P("tensor", None),
        P(),
        P(),
        P("expert", None, "tensor"),
        P("expert", None, "tensor"),
        P("expert", "tensor", None),
    )
    return jax.shard_map(
        shards,
        mesh=mesh,
        in_specs=placed,
        out_specs=(
            P("expert", "tensor"),
            P("expert", "tensor"),
            P(),
            P(None, "tensor"),
            P(None, "tensor"),
            P(None, "tensor"),
            P("tensor"),
            P("tensor"),
            P("tensor", None),
            P(),
            P(),
            P("expert", None, "tensor"),
            P("expert", None, "tensor"),
            P("expert", "tensor", None),
        ),
        check_vma=False,
    )
```

```python
import functools

import jax
import jax.numpy as jnp
from jax import lax
from jax.experimental import pallas as pl
from jax.experimental.pallas import tpu as pltpu
from jax.sharding import PartitionSpec as P


HD = 128
SLOT = 1024


EPS = 1e-05
THETA = 10000.0
NEGATIVE = -1e30


def cross_dot(operand, other_side):
    return lax.dot_general(
        operand, other_side, (((0,), (0,)), ((), ())), preferred_element_type=jnp.float32
    )


def dot_transposed(operand, other_side):
    return lax.dot_general(
        operand, other_side, (((1,), (1,)), ((), ())), preferred_element_type=jnp.float32
    )


def rotary_tables(length, head_size):
    frequency = THETA ** (-jnp.arange(0, head_size // 2, dtype=jnp.float32) * 2.0 / head_size)
    angles = jnp.arange(length, dtype=jnp.float32)[:, None] * frequency[None, :]
    return (jnp.cos(angles)[:, None, :], jnp.sin(angles)[:, None, :])


def rotate(values, cosine, sine_table):
    half_size = values.shape[-1] // 2
    first_half = values[..., :half_size]
    second = values[..., half_size:]
    return jnp.concatenate(
        [first_half * cosine - second * sine_table, second * cosine + first_half * sine_table],
        axis=-1,
    )


def unrotate(gradient, cosine, sine_table):
    half_size = gradient.shape[-1] // 2
    first_half = gradient[..., :half_size]
    second = gradient[..., half_size:]
    return jnp.concatenate(
        [first_half * cosine + second * sine_table, second * cosine - first_half * sine_table],
        axis=-1,
    )


def head_probs(q_ref, k_ref, length, start, stop):
    scores = dot_transposed(q_ref[start:stop, :], k_ref[:stop, :]) * HD ** (-0.5)
    query_pos = start + lax.broadcasted_iota(jnp.int32, scores.shape, 0)
    key_pos = lax.broadcasted_iota(jnp.int32, scores.shape, 1)
    allowed = (key_pos <= query_pos) & (key_pos < length)
    scores = jnp.where(allowed, scores, NEGATIVE)
    terms = jnp.exp(scores - jnp.max(scores, axis=1, keepdims=True))
    return terms / jnp.sum(terms, axis=1, keepdims=True)


def attend_body(length, q_ref, k_ref, v_ref, out_ref):
    rows = q_ref.shape[0]
    tile = rows // 4
    for start in range(0, rows, tile):
        stop = start + tile
        probs = head_probs(q_ref, k_ref, length[0], start, stop).astype(jnp.bfloat16)
        out_ref[start:stop, :] = jnp.dot(
            probs, v_ref[:stop, :], preferred_element_type=jnp.float32
        ).astype(jnp.bfloat16)


def attend_back_body(length, q_ref, k_ref, v_ref, d_ref, dq_ref, dk_ref, dv_ref, dv_sum):
    rows = q_ref.shape[0]
    tile = rows // 4
    for start in range(rows - tile, -1, -tile):
        stop = start + tile
        probs = head_probs(q_ref, k_ref, length[0], start, stop)
        d_block = d_ref[start:stop, :]
        d_probs = dot_transposed(d_block, v_ref[:stop, :])
        spread = jnp.sum(probs * d_probs, axis=1, keepdims=True)
        d_scores = (HD ** (-0.5) * probs * (d_probs - spread)).astype(jnp.bfloat16)
        dq_ref[start:stop, :] = jnp.dot(
            d_scores, k_ref[:stop, :], preferred_element_type=jnp.float32
        )
        d_keys = cross_dot(d_scores, q_ref[start:stop, :])
        d_values = cross_dot(probs.astype(jnp.bfloat16), d_block)
        if stop == rows:
            dk_ref[...] = d_keys
            dv_sum[...] = d_values
        else:
            dk_ref[:stop, :] += d_keys
            dv_sum[:stop, :] += d_values
    dv_ref[...] = dv_sum[...].astype(jnp.bfloat16)


def per_head(body, lengths, operands, out_types, scratch):
    rows, width = operands[0].shape
    block = pl.BlockSpec((rows, HD), lambda h, *_: (0, h))
    return pl.pallas_call(
        body,
        out_shape=[jax.ShapeDtypeStruct((rows, width), t) for t in out_types],
        grid_spec=pltpu.PrefetchScalarGridSpec(
            num_scalar_prefetch=1,
            grid=(width // HD,),
            in_specs=[block] * len(operands),
            out_specs=[block] * len(out_types),
            scratch_shapes=scratch,
        ),
    )(lengths, *operands)


def act_body(
    n_local,
    n_before,
    meta,
    x_near,
    x_far,
    g_near,
    g_far,
    info_ref,
    gate_up_own,
    gate_up_other,
    down_own,
    down_other,
    *rest,
):
    outs = rest[n_before:]
    out_refs, back_refs = outs[:2], outs[2:4]
    x_all, g_all, pre_own, pre_other, inner_own, inner_other, dgate_ref, staged = outs[4:]
    cols = x_near.shape[2]
    hidden = down_own.shape[0]
    width = hidden // n_local
    place = meta[0]

    def columns(core, across):
        return pl.ds(pl.multiple_of((place ^ (core + 2 * across)) * cols, cols), cols)

    def spread(pieces, target):
        for core in range(2):
            for across in range(2):
                target[:, columns(core, across)] = pieces[core][across]

    def collect(value, targets):
        staged[...] = value.astype(jnp.bfloat16)
        for core in range(2):
            for across in range(2):
                targets[core][across] = staged[:, columns(core, across)]

    spread((x_near, x_far), x_all)
    spread((g_near, g_far), g_all)
    live = meta[1] < meta[2 + pl.program_id(0)]

    @pl.when(live)
    def _():
        scale = info_ref[:, n_local : n_local + 1]
        dgate = [None] * n_local
        out, back = None, None
        for gate_up, down, pre_ref, inner_ref in (
            (gate_up_own, down_own, pre_own, inner_own),
            (gate_up_other, down_other, pre_other, inner_other),
        ):
            pre = jnp.dot(x_all[...], gate_up[...], preferred_element_type=jnp.float32)
            d_raw = dot_transposed(g_all[...], down[...])
            for e in range(n_local):
                at = slice(e * width, (e + 1) * width)
                up_at = slice(hidden + e * width, hidden + (e + 1) * width)
                gate_pre = pre[:, at] * scale
                up_pre = pre[:, up_at] * scale
                gate = info_ref[:, e : e + 1]
                sigma = jax.nn.sigmoid(gate_pre)
                silu_value = gate_pre * sigma
                inner = silu_value * up_pre
                raw = d_raw[:, at]
                share = jnp.sum(inner * raw, axis=1, keepdims=True)
                dgate[e] = share if dgate[e] is None else dgate[e] + share
                d_inner = raw * (gate * scale)
                inner_ref[:, at] = (inner * gate).astype(jnp.bfloat16)
                pre_ref[:, at] = (
                    d_inner * up_pre * sigma * (1.0 + gate_pre * (1.0 - sigma))
                ).astype(jnp.bfloat16)
                pre_ref[:, up_at] = (d_inner * silu_value).astype(jnp.bfloat16)
            out_part = jnp.dot(inner_ref[...], down[...], preferred_element_type=jnp.float32)
            back_part = dot_transposed(pre_ref[...], gate_up[...])
            out = out_part if out is None else out + out_part
            back = back_part if back is None else back + back_part
        for e in range(n_local):
            dgate_ref[:, e : e + 1] = dgate[e]
        collect(out, out_refs)
        collect(back, back_refs)

    @pl.when(jnp.logical_not(live))
    def _():
        for ref in (pre_own, pre_other, inner_own, inner_other, dgate_ref):
            ref[...] = jnp.zeros_like(ref)
        for ref in (*out_refs, *back_refs):
            ref[...] = jnp.zeros_like(ref)


def act_call(step, n_steps, meta, x_pair, g_pair, info, weights, n_local, before):
    slots, pieces, rows, cols = x_pair[0].shape
    model = 2 * pieces * cols
    hidden = weights[2].shape[0]
    bf16 = jnp.bfloat16
    piece = pl.BlockSpec((None, pieces, rows, cols), lambda s, *_: (s, 0, 0, 0))
    g_piece = pl.BlockSpec((None, pieces, rows, cols), lambda s, *_: (s, 0, step, 0))
    info_rows = pl.BlockSpec((None, rows, info.shape[2]), lambda s, *_: (s, 0, 0))

    def stacked(minor):
        return pl.BlockSpec((None, None, rows, minor), lambda s, *_: (step, s, 0, 0))

    def whole(array):
        return pl.BlockSpec(array.shape, lambda s, *_: (0, 0), pipeline_mode=pl.Buffered(1))

    part = jax.ShapeDtypeStruct(x_pair[0].shape, bf16)
    minors = (model, model, 2 * hidden, 2 * hidden, hidden, hidden)
    stacks = tuple(jax.ShapeDtypeStruct((n_steps, slots, rows, m), bf16) for m in minors)
    results = pl.pallas_call(
        functools.partial(act_body, n_local, len(before)),
        out_shape=(part,) * 4 + stacks + (jax.ShapeDtypeStruct(info.shape, jnp.float32),),
        grid_spec=pltpu.PrefetchScalarGridSpec(
            num_scalar_prefetch=1,
            grid=(slots,),
            in_specs=[piece, piece, g_piece, g_piece, info_rows]
            + [whole(w) for w in weights]
            + [pl.BlockSpec(memory_space=pl.ANY)] * len(before),
            out_specs=[piece] * 4 + [stacked(m) for m in minors] + [info_rows],
            scratch_shapes=[pltpu.VMEM((rows, model), bf16)],
        ),
        input_output_aliases={10 + i: 4 + i for i in range(len(before))},
        name="experts",
    )(meta, *x_pair, *g_pair, info, *weights, *before)
    return results[:2], results[2:4], results[4:10], results[10]


def layer(
    block_input,
    cotangent,
    lengths,
    routes,
    g_attn,
    w_query,
    w_key,
    w_value,
    g_query,
    g_key,
    w_out,
    g_moe,
    w_router,
    w_gate,
    w_up,
    w_down,
):
    tok_rows, slice_width = block_input.shape
    n_tensor = lax.axis_size("tensor")
    n_expert = lax.axis_size("expert")
    model_width = slice_width * n_tensor
    n_experts = w_router.shape[1]
    n_local = w_gate.shape[0]
    heads_here = w_query.shape[1] // HD
    e_index = lax.axis_index("expert")
    offset = lax.axis_index("tensor") * slice_width
    t_index = lax.axis_index("tensor")
    x_index = t_index // 2
    n_steps = 2
    half = tok_rows // 2
    stripe = tok_rows // 8
    f32, bf16 = jnp.float32, jnp.bfloat16

    def over_core(v):
        return lax.ppermute(v, "tensor", [(i, i ^ 1) for i in range(n_tensor)])

    def over_x(v):
        return lax.ppermute(v, "tensor", [(i, i ^ 2) for i in range(n_tensor)])

    def over_y(v):
        return lax.ppermute(v, "expert", [(i, i ^ 1) for i in range(n_expert)])

    def over_z(v):
        return lax.ppermute(v, "expert", [(i, (i + 2) % n_expert) for i in range(n_expert)])

    def tensor_sum(v):
        v = v + over_core(v)
        return v + over_x(v)

    def striped(v, index):
        parts = v.reshape((-1, 2, stripe) + v.shape[1:])
        return lax.dynamic_index_in_dim(parts, index, 1, False).reshape((half,) + v.shape[1:])

    def unstriped(mine, other):
        shape = (-1, 1, stripe) + mine.shape[1:]
        a = jnp.where(x_index == 0, mine, other).reshape(shape)
        b = jnp.where(x_index == 0, other, mine).reshape(shape)
        return jnp.concatenate([a, b], axis=1).reshape((tok_rows,) + mine.shape[1:])

    def exchanged(rows):
        return jnp.stack([striped(rows, x_index), over_x(striped(rows, 1 - x_index))])

    def joined(parts):
        near, far = parts
        return (near.astype(f32) + over_core(far).astype(f32)).astype(bf16)

    def reduced(message):
        return lax.psum_scatter(message, "expert", scatter_dimension=0)

    def home(total):
        return unstriped(total[0].astype(f32), over_x(total[1]).astype(f32))

    def expert_sum(grad):
        rows, cols = grad.shape
        n_z, z_index, y_index = n_expert // 2, e_index // 2, e_index % 2
        parts = grad.astype(bf16).reshape(2, n_z, rows // n_expert, cols)
        sent = over_y(lax.dynamic_index_in_dim(parts, 1 - y_index, 0, False))
        kept = lax.dynamic_index_in_dim(parts, y_index, 0, False)
        kept = kept.astype(f32) + sent.astype(f32)
        carried = None
        for step in [*range(1, n_z), 0]:
            at = lax.rem(z_index + n_z - step, n_z)
            total = lax.dynamic_index_in_dim(kept, at, 0, False)
            if carried is not None:
                total = total + carried.astype(f32)
            if step:
                carried = over_z(total.astype(bf16))
        near = [total.astype(bf16)]
        for _ in range(1, n_z):
            near.append(over_z(near[-1]))
        far = [over_y(v) for v in near]

        def ordered(pieces):
            pieces = pieces[::-1]
            doubled = jnp.concatenate(pieces + pieces[:-1], axis=0)
            start = (n_z - 1 - z_index) * (rows // n_expert)
            return lax.dynamic_slice_in_dim(doubled, start, rows // 2, 0)

        near, far = ordered(near), ordered(far)
        first = y_index == 0
        return jnp.concatenate(
            [jnp.where(first, near, far), jnp.where(first, far, near)], axis=0
        ).astype(f32)

    def column_parts(make):
        p0, p1, p2, p3 = [make((t_index ^ p) * slice_width) for p in range(4)]
        mine = p0 + over_core(p1.astype(bf16)).astype(f32)
        other = p2 + over_core(p3.astype(bf16)).astype(f32)
        return mine + over_x(other.astype(bf16)).astype(f32)

    def own_columns(vector):
        return lax.dynamic_slice_in_dim(vector, offset, slice_width, vector.ndim - 1)

    full_input = lax.all_gather(block_input, "tensor", axis=1, tiled=True)
    own_gu = jnp.concatenate(
        [w_gate[e] for e in range(n_local)] + [w_up[e] for e in range(n_local)], axis=1
    )
    own_down = w_down.reshape(-1, model_width)
    early_gu, early_down, early_dy, _ = lax.optimization_barrier(
        (own_gu, own_down, cotangent, full_input)
    )
    dy_near = lax.all_gather(exchanged(early_dy), "expert", axis=0)
    mats = (own_gu, over_x(early_gu), own_down, over_x(early_down))
    positions = jnp.arange(tok_rows)
    live_rows = positions < lengths[0]
    valid_rows = live_rows.astype(jnp.float32)[:, None]
    input_full = full_input.astype(jnp.float32)
    scale_x = lax.rsqrt(jnp.mean(input_full * input_full, axis=-1, keepdims=True) + EPS)
    normed = (input_full * scale_x * g_attn).astype(jnp.bfloat16)
    q_raw = jnp.dot(normed, w_query, preferred_element_type=jnp.float32)
    k_raw = jnp.dot(normed, w_key, preferred_element_type=jnp.float32)
    values = jnp.dot(normed, w_value, preferred_element_type=jnp.float32).astype(jnp.bfloat16)
    q_total, k_total = tensor_sum(
        jnp.stack([jnp.sum(q_raw * q_raw, axis=1), jnp.sum(k_raw * k_raw, axis=1)])
    )
    scale_q = lax.rsqrt(q_total / model_width + EPS)[:, None]
    scale_k = lax.rsqrt(k_total / model_width + EPS)[:, None]
    q_norm = q_raw * scale_q * g_query
    k_norm = k_raw * scale_k * g_key
    cosine, sine_table = rotary_tables(SLOT, HD)
    head_shape = (SLOT, heads_here, HD)
    flat_shape = (tok_rows, heads_here * HD)
    query = rotate(q_norm.reshape(head_shape), cosine, sine_table).astype(bf16).reshape(flat_shape)
    keys = rotate(k_norm.reshape(head_shape), cosine, sine_table).astype(bf16).reshape(flat_shape)
    (heads_out,) = per_head(attend_body, lengths, (query, keys, values), [bf16], [])
    attn_slice = column_parts(
        lambda at: jnp.dot(
            heads_out,
            lax.dynamic_slice_in_dim(w_out, at, slice_width, 1),
            preferred_element_type=f32,
        )
    )
    hidden = block_input.astype(f32) + attn_slice
    g_moe_slice = own_columns(g_moe)
    moe_rows = (hidden * g_moe_slice).astype(jnp.bfloat16)
    moe_piece = exchanged(moe_rows)
    moe_piece, dy_near = lax.optimization_barrier((moe_piece, dy_near))
    x_near = [
        lax.all_gather(v, "expert", axis=0) for v in jnp.split(moe_piece, n_steps, axis=1)
    ]
    router_slice = lax.dynamic_slice_in_dim(w_router, offset, slice_width, 0)
    statistics = jnp.concatenate(
        [
            jnp.dot(moe_rows, router_slice, preferred_element_type=jnp.float32),
            jnp.sum(hidden * hidden, axis=1, keepdims=True),
        ],
        axis=1,
    )
    statistics = tensor_sum(statistics.T).T
    scale_h = lax.rsqrt(statistics[:, n_experts:] / model_width + EPS)
    router_probs = jax.nn.softmax(statistics[:, :n_experts] * scale_h, axis=-1)
    expert_ids = jnp.arange(n_experts, dtype=jnp.int32)
    chosen = jnp.any(routes[:, :, None] == expert_ids[None, None, :], axis=1) & live_rows[:, None]
    chosen = chosen.astype(jnp.float32)
    gates = router_probs * chosen
    flat = jnp.concatenate(
        [
            gates.T,
            scale_h.T,
            jnp.full((1, tok_rows), lengths[0].astype(f32)),
            jnp.zeros((6, tok_rows), f32),
        ],
        axis=0,
    )
    flat = lax.all_gather(flat, "expert", axis=0)
    all_lengths = flat[:, n_experts + 1, 0].astype(jnp.int32)
    info = jnp.concatenate(
        [
            lax.dynamic_slice_in_dim(flat, e_index * n_local, n_local, 1),
            flat[:, n_experts : n_experts + 1],
            jnp.zeros((n_expert, 8 - n_local - 1, tok_rows), f32),
        ],
        axis=1,
    )
    info = lax.dynamic_index_in_dim(info.reshape(n_expert, 8, -1, 2, stripe), x_index, 3, False)
    info = info.reshape(n_expert, 8, n_steps, -1).transpose(2, 0, 3, 1)
    part_rows = half // n_steps

    dy_pair = (dy_near, over_core(dy_near))
    out_parts, back_parts, extras, stacks = [], [], [], ()
    for step in range(n_steps):
        first = step * 2 * part_rows + x_index * stripe
        meta = jnp.concatenate([jnp.stack([t_index, first]), all_lengths])
        x_pair = (x_near[step], over_core(x_near[step]))
        outs, backs, stacks, dgate = act_call(
            step, n_steps, meta, x_pair, dy_pair, info[step], mats, n_local, stacks
        )
        out_parts.append(outs)
        rows = lax.dynamic_update_slice_in_dim(
            jnp.zeros((n_expert, n_experts, slice_width), f32),
            jnp.pad(
                dgate[:, :, :n_local].transpose(0, 2, 1),
                ((0, 0), (0, 0), (0, slice_width - part_rows)),
            ),
            e_index * n_local,
            1,
        )
        high = lax.reduce_precision(rows, 8, 7)
        extra = jnp.stack([high, rows - high], axis=1).astype(bf16)
        total = reduced(jnp.concatenate([joined(backs), extra], axis=2))
        back_parts.append(total[:, :part_rows])
        extra = total[:, part_rows:, :part_rows].astype(f32)
        extras.append(extra[0] + extra[1])
    x_stack, g_stack, pre_own, pre_other, inner_own, inner_other = [
        v.reshape(-1, v.shape[3]) for v in stacks
    ]
    other_gu = cross_dot(x_stack, pre_other).astype(bf16)
    other_down = cross_dot(inner_other, g_stack).astype(bf16)
    mine_gu = cross_dot(x_stack, pre_own)
    mine_down = cross_dot(inner_own, g_stack)
    out_message = jnp.concatenate([joined(parts) for parts in out_parts], axis=2)
    back_total = jnp.concatenate(back_parts, axis=1)
    back_total, out_message, other_gu, other_down, mine_gu, mine_down = lax.optimization_barrier(
        (back_total, out_message, other_gu, other_down, mine_gu, mine_down)
    )
    back_slice = home(back_total)
    moe_total = reduced(out_message)

    total = jnp.concatenate(extras, axis=1)
    total = total + over_core(total)
    d_gates = unstriped(total.T, over_x(total).T)

    d_probs = d_gates * chosen
    d_logits = (
        router_probs * (d_probs - jnp.sum(router_probs * d_probs, axis=-1, keepdims=True))
    ).astype(jnp.bfloat16)
    scaled_logits = (d_logits.astype(jnp.float32) * scale_h).astype(jnp.bfloat16)
    router_grad = cross_dot(moe_rows, scaled_logits)
    back_slice = back_slice + dot_transposed(scaled_logits, router_slice)
    projection = jnp.sum(back_slice * (hidden * g_moe_slice), axis=1)
    h_term = (tensor_sum(projection[None])[0] / model_width)[:, None] * scale_h * scale_h
    d_out_slice = cotangent.astype(f32) * valid_rows
    d_hidden_slice = d_out_slice + g_moe_slice * back_slice - hidden * h_term
    grad_g_moe = jnp.sum(back_slice * hidden, axis=0)
    d_attn = d_hidden_slice.astype(bf16)
    across = over_x(d_attn)
    d_attn = [d_attn, over_core(d_attn), across, over_core(across)]
    grad_w_out = jnp.concatenate([cross_dot(heads_out, v) for v in d_attn], axis=1)
    d_heads = sum(
        dot_transposed(
            v, lax.dynamic_slice_in_dim(w_out, (t_index ^ p) * slice_width, slice_width, 1)
        )
        for p, v in enumerate(d_attn)
    )
    d_heads = d_heads.astype(bf16)
    other_gu, other_down, _ = lax.optimization_barrier((other_gu, other_down, d_attn[3]))
    other_gu, other_down = over_x(other_gu), over_x(other_down)
    d_query, d_keys, d_values = per_head(
        attend_back_body,
        lengths,
        (query, keys, values, d_heads),
        [f32, f32, bf16],
        [pltpu.VMEM((tok_rows, HD), f32)],
    )
    d_q_norm = unrotate(d_query.reshape(head_shape), cosine, sine_table).reshape(tok_rows, heads_here * HD)
    d_k_norm = unrotate(d_keys.reshape(head_shape), cosine, sine_table).reshape(tok_rows, heads_here * HD)
    q_sum, k_sum = tensor_sum(
        jnp.stack(
            [jnp.sum(d_q_norm * g_query * q_raw, axis=1), jnp.sum(d_k_norm * g_key * k_raw, axis=1)]
        )
    )
    grad_g_query = jnp.sum(d_q_norm * q_raw * scale_q, axis=0)
    grad_g_key = jnp.sum(d_k_norm * k_raw * scale_k, axis=0)
    d_q_raw = (
        scale_q * g_query * d_q_norm - q_raw * scale_q**3 * (q_sum / model_width)[:, None]
    ).astype(jnp.bfloat16)
    d_k_raw = (
        scale_k * g_key * d_k_norm - k_raw * scale_k**3 * (k_sum / model_width)[:, None]
    ).astype(jnp.bfloat16)
    grad_w_query = cross_dot(normed, d_q_raw)
    grad_w_key = cross_dot(normed, d_k_raw)
    grad_w_value = cross_dot(normed, d_values)

    def normed_columns(at):
        def back(gradient, weight):
            return dot_transposed(gradient, lax.dynamic_slice_in_dim(weight, at, slice_width, 0))

        return back(d_q_raw, w_query) + back(d_k_raw, w_key) + back(d_values, w_value)

    column_sums = jnp.sum(
        d_q_raw.astype(jnp.float32) * q_raw
        + d_k_raw.astype(jnp.float32) * k_raw
        + d_values.astype(jnp.float32) * values.astype(jnp.float32),
        axis=1,
    )
    x_mean = (tensor_sum(column_sums[None])[0] / model_width)[:, None]
    d_normed = column_parts(normed_columns)
    x_hat = block_input.astype(jnp.float32) * scale_x
    grad_g_attn = jnp.sum(d_normed * x_hat, axis=0)
    grad_input = (
        d_hidden_slice + scale_x * (d_normed * own_columns(g_attn) - x_hat * x_mean)
    ).astype(jnp.bfloat16)

    sum_query, sum_key, sum_value = map(expert_sum, (grad_w_query, grad_w_key, grad_w_value))
    ready, moe_total = lax.optimization_barrier((grad_w_out.astype(bf16), moe_total))
    sum_out = lax.psum(ready, "expert").astype(f32)
    moe_slice = home(moe_total)
    output = (valid_rows * (hidden + moe_slice)).astype(bf16)
    sum_out = jnp.concatenate(
        [
            lax.dynamic_slice_in_dim(sum_out, (t_index ^ p) * slice_width, slice_width, 1)
            for p in range(4)
        ],
        axis=1,
    )
    other_gu, other_down, _ = lax.optimization_barrier((other_gu, other_down, d_k_raw))
    grad_gu = mine_gu + other_gu.astype(f32)
    grad_w_down = (mine_down + other_down.astype(f32)).reshape(w_down.shape)
    grad_gu = grad_gu.reshape(model_width, 2, n_local, -1)
    grad_w_gate = grad_gu[:, 0].transpose(1, 0, 2)
    grad_w_up = grad_gu[:, 1].transpose(1, 0, 2)
    small = jnp.concatenate(
        [router_grad.T, grad_g_moe[None], grad_g_attn[None], grad_g_query[None], grad_g_key[None]],
        axis=0,
    )
    hop = 1
    while hop < n_expert:
        small = small + lax.ppermute(small, "expert", [(i, i ^ hop) for i in range(n_expert)])
        hop *= 2
    shared = tensor_sum(
        lax.dynamic_update_slice_in_dim(
            jnp.zeros((n_experts + 2, model_width), f32), small[: n_experts + 2], offset, 1
        )
    )
    return (
        output,
        grad_input,
        shared[n_experts + 1],
        sum_query,
        sum_key,
        sum_value,
        small[n_experts + 2],
        small[n_experts + 3],
        sum_out,
        shared[n_experts],
        shared[:n_experts].T,
        grad_w_gate,
        grad_w_up,
        grad_w_down,
    )


def solution(mesh):
    placed = (
        P("expert", "tensor"),
        P("expert", "tensor"),
        P("expert"),
        P("expert", None),
        P(),
        P(None, "tensor"),
        P(None, "tensor"),
        P(None, "tensor"),
        P("tensor"),
        P("tensor"),
        P("tensor", None),
        P(),
        P(),
        P("expert", None, "tensor"),
        P("expert", None, "tensor"),
        P("expert", "tensor", None),
    )
    return jax.shard_map(
        layer,
        mesh=mesh,
        in_specs=placed,
        out_specs=(
            P("expert", "tensor"),
            P("expert", "tensor"),
            P(),
            P(None, "tensor"),
            P(None, "tensor"),
            P(None, "tensor"),
            P("tensor"),
            P("tensor"),
            P("tensor", None),
            P(),
            P(),
            P("expert", None, "tensor"),
            P("expert", None, "tensor"),
            P("expert", "tensor", None),
        ),
        check_vma=False,
    )
```

```python
import functools

import jax
import jax.numpy as jnp
from jax import lax
from jax.experimental import pallas as pl
from jax.experimental.pallas import tpu as pltpu
from jax.sharding import PartitionSpec as P


HD = 128
SLOT = 1024


EPS = 1e-05
THETA = 10000.0
NEGATIVE = -1e30


def cross_dot(operand, other_side):
    return lax.dot_general(
        operand, other_side, (((0,), (0,)), ((), ())), preferred_element_type=jnp.float32
    )


def dot_transposed(operand, other_side):
    return lax.dot_general(
        operand, other_side, (((1,), (1,)), ((), ())), preferred_element_type=jnp.float32
    )


def rotary_tables(length, head_size):
    frequency = THETA ** (-jnp.arange(0, head_size // 2, dtype=jnp.float32) * 2.0 / head_size)
    angles = jnp.arange(length, dtype=jnp.float32)[:, None] * frequency[None, :]
    return (jnp.cos(angles)[:, None, :], jnp.sin(angles)[:, None, :])


def rotate(values, cosine, sine_table):
    half_size = values.shape[-1] // 2
    first_half = values[..., :half_size]
    second = values[..., half_size:]
    return jnp.concatenate(
        [first_half * cosine - second * sine_table, second * cosine + first_half * sine_table],
        axis=-1,
    )


def unrotate(gradient, cosine, sine_table):
    half_size = gradient.shape[-1] // 2
    first_half = gradient[..., :half_size]
    second = gradient[..., half_size:]
    return jnp.concatenate(
        [first_half * cosine + second * sine_table, second * cosine - first_half * sine_table],
        axis=-1,
    )


def head_probs(q_ref, k_ref, length, start, stop):
    scores = dot_transposed(q_ref[start:stop, :], k_ref[:stop, :]) * HD ** (-0.5)
    query_pos = start + lax.broadcasted_iota(jnp.int32, scores.shape, 0)
    key_pos = lax.broadcasted_iota(jnp.int32, scores.shape, 1)
    allowed = (key_pos <= query_pos) & (key_pos < length)
    scores = jnp.where(allowed, scores, NEGATIVE)
    terms = jnp.exp(scores - jnp.max(scores, axis=1, keepdims=True))
    return terms / jnp.sum(terms, axis=1, keepdims=True)


def attend_body(length, q_ref, k_ref, v_ref, out_ref):
    rows = q_ref.shape[0]
    tile = rows // 4
    for start in range(0, rows, tile):
        stop = start + tile
        probs = head_probs(q_ref, k_ref, length[0], start, stop).astype(jnp.bfloat16)
        out_ref[start:stop, :] = jnp.dot(
            probs, v_ref[:stop, :], preferred_element_type=jnp.float32
        ).astype(jnp.bfloat16)


def attend_back_body(length, q_ref, k_ref, v_ref, d_ref, dq_ref, dk_ref, dv_ref, dv_sum):
    rows = q_ref.shape[0]
    tile = rows // 4
    for start in range(rows - tile, -1, -tile):
        stop = start + tile
        probs = head_probs(q_ref, k_ref, length[0], start, stop)
        d_block = d_ref[start:stop, :]
        d_probs = dot_transposed(d_block, v_ref[:stop, :])
        spread = jnp.sum(probs * d_probs, axis=1, keepdims=True)
        d_scores = (HD ** (-0.5) * probs * (d_probs - spread)).astype(jnp.bfloat16)
        dq_ref[start:stop, :] = jnp.dot(
            d_scores, k_ref[:stop, :], preferred_element_type=jnp.float32
        )
        d_keys = cross_dot(d_scores, q_ref[start:stop, :])
        d_values = cross_dot(probs.astype(jnp.bfloat16), d_block)
        if stop == rows:
            dk_ref[...] = d_keys
            dv_sum[...] = d_values
        else:
            dk_ref[:stop, :] += d_keys
            dv_sum[:stop, :] += d_values
    dv_ref[...] = dv_sum[...].astype(jnp.bfloat16)


def per_head(body, lengths, operands, out_types, scratch):
    rows, width = operands[0].shape
    block = pl.BlockSpec((rows, HD), lambda h, *_: (0, h))
    return pl.pallas_call(
        body,
        out_shape=[jax.ShapeDtypeStruct((rows, width), t) for t in out_types],
        grid_spec=pltpu.PrefetchScalarGridSpec(
            num_scalar_prefetch=1,
            grid=(width // HD,),
            in_specs=[block] * len(operands),
            out_specs=[block] * len(out_types),
            scratch_shapes=scratch,
        ),
    )(lengths, *operands)


def act_body(
    n_local,
    n_before,
    meta,
    x_near,
    x_far,
    g_near,
    g_far,
    info_ref,
    gate_up_own,
    gate_up_other,
    down_own,
    down_other,
    *rest,
):
    outs = rest[n_before:]
    out_refs, back_refs = outs[:2], outs[2:4]
    x_all, g_all, pre_own, pre_other, inner_own, inner_other, dgate_ref, staged = outs[4:]
    cols = x_near.shape[2]
    hidden = down_own.shape[0]
    width = hidden // n_local
    place = meta[0]

    def columns(core, across):
        return pl.ds(pl.multiple_of((place ^ (core + 2 * across)) * cols, cols), cols)

    def spread(pieces, target):
        for core in range(2):
            for across in range(2):
                target[:, columns(core, across)] = pieces[core][across]

    def collect(value, targets):
        staged[...] = value.astype(jnp.bfloat16)
        for core in range(2):
            for across in range(2):
                targets[core][across] = staged[:, columns(core, across)]

    spread((x_near, x_far), x_all)
    spread((g_near, g_far), g_all)
    live = meta[1] < meta[2 + pl.program_id(0)]

    @pl.when(live)
    def _():
        scale = info_ref[:, n_local : n_local + 1]
        dgate = [None] * n_local
        out, back = None, None
        for gate_up, down, pre_ref, inner_ref in (
            (gate_up_own, down_own, pre_own, inner_own),
            (gate_up_other, down_other, pre_other, inner_other),
        ):
            pre = jnp.dot(x_all[...], gate_up[...], preferred_element_type=jnp.float32)
            d_raw = dot_transposed(g_all[...], down[...])
            for e in range(n_local):
                at = slice(e * width, (e + 1) * width)
                up_at = slice(hidden + e * width, hidden + (e + 1) * width)
                gate_pre = pre[:, at] * scale
                up_pre = pre[:, up_at] * scale
                gate = info_ref[:, e : e + 1]
                sigma = jax.nn.sigmoid(gate_pre)
                silu_value = gate_pre * sigma
                inner = silu_value * up_pre
                raw = d_raw[:, at]
                share = jnp.sum(inner * raw, axis=1, keepdims=True)
                dgate[e] = share if dgate[e] is None else dgate[e] + share
                d_inner = raw * (gate * scale)
                inner_ref[:, at] = (inner * gate).astype(jnp.bfloat16)
                pre_ref[:, at] = (
                    d_inner * up_pre * sigma * (1.0 + gate_pre * (1.0 - sigma))
                ).astype(jnp.bfloat16)
                pre_ref[:, up_at] = (d_inner * silu_value).astype(jnp.bfloat16)
            out_part = jnp.dot(inner_ref[...], down[...], preferred_element_type=jnp.float32)
            back_part = dot_transposed(pre_ref[...], gate_up[...])
            out = out_part if out is None else out + out_part
            back = back_part if back is None else back + back_part
        for e in range(n_local):
            dgate_ref[:, e : e + 1] = dgate[e]
        collect(out, out_refs)
        collect(back, back_refs)

    @pl.when(jnp.logical_not(live))
    def _():
        for ref in (pre_own, pre_other, inner_own, inner_other, dgate_ref):
            ref[...] = jnp.zeros_like(ref)
        for ref in (*out_refs, *back_refs):
            ref[...] = jnp.zeros_like(ref)


def act_call(step, n_steps, meta, x_pair, g_pair, info, weights, n_local, before):
    slots, pieces, rows, cols = x_pair[0].shape
    model = 2 * pieces * cols
    hidden = weights[2].shape[0]
    bf16 = jnp.bfloat16
    piece = pl.BlockSpec((None, pieces, rows, cols), lambda s, *_: (s, 0, 0, 0))
    g_piece = pl.BlockSpec((None, pieces, rows, cols), lambda s, *_: (s, 0, step, 0))
    info_rows = pl.BlockSpec((None, rows, info.shape[2]), lambda s, *_: (s, 0, 0))

    def stacked(minor):
        return pl.BlockSpec((None, None, rows, minor), lambda s, *_: (step, s, 0, 0))

    def whole(array):
        return pl.BlockSpec(array.shape, lambda s, *_: (0, 0), pipeline_mode=pl.Buffered(1))

    part = jax.ShapeDtypeStruct(x_pair[0].shape, bf16)
    minors = (model, model, 2 * hidden, 2 * hidden, hidden, hidden)
    stacks = tuple(jax.ShapeDtypeStruct((n_steps, slots, rows, m), bf16) for m in minors)
    results = pl.pallas_call(
        functools.partial(act_body, n_local, len(before)),
        out_shape=(part,) * 4 + stacks + (jax.ShapeDtypeStruct(info.shape, jnp.float32),),
        grid_spec=pltpu.PrefetchScalarGridSpec(
            num_scalar_prefetch=1,
            grid=(slots,),
            in_specs=[piece, piece, g_piece, g_piece, info_rows]
            + [whole(w) for w in weights]
            + [pl.BlockSpec(memory_space=pl.ANY)] * len(before),
            out_specs=[piece] * 4 + [stacked(m) for m in minors] + [info_rows],
            scratch_shapes=[pltpu.VMEM((rows, model), bf16)],
        ),
        input_output_aliases={10 + i: 4 + i for i in range(len(before))},
        name="experts",
    )(meta, *x_pair, *g_pair, info, *weights, *before)
    return results[:2], results[2:4], results[4:10], results[10]


def layer(
    block_input,
    cotangent,
    lengths,
    routes,
    g_attn,
    w_query,
    w_key,
    w_value,
    g_query,
    g_key,
    w_out,
    g_moe,
    w_router,
    w_gate,
    w_up,
    w_down,
):
    tok_rows, slice_width = block_input.shape
    n_tensor = lax.axis_size("tensor")
    n_expert = lax.axis_size("expert")
    model_width = slice_width * n_tensor
    n_experts = w_router.shape[1]
    n_local = w_gate.shape[0]
    heads_here = w_query.shape[1] // HD
    e_index = lax.axis_index("expert")
    offset = lax.axis_index("tensor") * slice_width
    t_index = lax.axis_index("tensor")
    x_index = t_index // 2
    n_steps = 2
    half = tok_rows // 2
    stripe = tok_rows // 8
    f32, bf16 = jnp.float32, jnp.bfloat16

    def over_core(v):
        return lax.ppermute(v, "tensor", [(i, i ^ 1) for i in range(n_tensor)])

    def over_x(v):
        return lax.ppermute(v, "tensor", [(i, i ^ 2) for i in range(n_tensor)])

    def over_y(v):
        return lax.ppermute(v, "expert", [(i, i ^ 1) for i in range(n_expert)])

    def over_z(v):
        return lax.ppermute(v, "expert", [(i, (i + 2) % n_expert) for i in range(n_expert)])

    def tensor_sum(v):
        v = v + over_core(v)
        return v + over_x(v)

    def striped(v, index):
        parts = v.reshape((-1, 2, stripe) + v.shape[1:])
        return lax.dynamic_index_in_dim(parts, index, 1, False).reshape((half,) + v.shape[1:])

    def unstriped(mine, other):
        shape = (-1, 1, stripe) + mine.shape[1:]
        a = jnp.where(x_index == 0, mine, other).reshape(shape)
        b = jnp.where(x_index == 0, other, mine).reshape(shape)
        return jnp.concatenate([a, b], axis=1).reshape((tok_rows,) + mine.shape[1:])

    def exchanged(rows):
        return jnp.stack([striped(rows, x_index), over_x(striped(rows, 1 - x_index))])

    def joined(parts):
        near, far = parts
        return (near.astype(f32) + over_core(far).astype(f32)).astype(bf16)

    def reduced(message):
        return lax.psum_scatter(message, "expert", scatter_dimension=0)

    def home(total):
        return unstriped(total[0].astype(f32), over_x(total[1]).astype(f32))

    def expert_sum(grad):
        rows, cols = grad.shape
        n_z, z_index, y_index = n_expert // 2, e_index // 2, e_index % 2
        parts = grad.astype(bf16).reshape(2, n_z, rows // n_expert, cols)
        sent = over_y(lax.dynamic_index_in_dim(parts, 1 - y_index, 0, False))
        kept = lax.dynamic_index_in_dim(parts, y_index, 0, False)
        kept = kept.astype(f32) + sent.astype(f32)
        carried = None
        for step in [*range(1, n_z), 0]:
            at = lax.rem(z_index + n_z - step, n_z)
            total = lax.dynamic_index_in_dim(kept, at, 0, False)
            if carried is not None:
                total = total + carried.astype(f32)
            if step:
                carried = over_z(total.astype(bf16))
        near = [total.astype(bf16)]
        for _ in range(1, n_z):
            near.append(over_z(near[-1]))
        far = [over_y(v) for v in near]

        def ordered(pieces):
            pieces = pieces[::-1]
            doubled = jnp.concatenate(pieces + pieces[:-1], axis=0)
            start = (n_z - 1 - z_index) * (rows // n_expert)
            return lax.dynamic_slice_in_dim(doubled, start, rows // 2, 0)

        near, far = ordered(near), ordered(far)
        first = y_index == 0
        return jnp.concatenate(
            [jnp.where(first, near, far), jnp.where(first, far, near)], axis=0
        ).astype(f32)

    def column_parts(make):
        p0, p1, p2, p3 = [make((t_index ^ p) * slice_width) for p in range(4)]
        mine = p0 + over_core(p1.astype(bf16)).astype(f32)
        other = p2 + over_core(p3.astype(bf16)).astype(f32)
        return mine + over_x(other.astype(bf16)).astype(f32)

    def own_columns(vector):
        return lax.dynamic_slice_in_dim(vector, offset, slice_width, vector.ndim - 1)

    full_input = lax.all_gather(block_input, "tensor", axis=1, tiled=True)
    own_gu = jnp.concatenate(
        [w_gate[e] for e in range(n_local)] + [w_up[e] for e in range(n_local)], axis=1
    )
    own_down = w_down.reshape(-1, model_width)
    early_gu, early_down, early_dy, _ = lax.optimization_barrier(
        (own_gu, own_down, cotangent, full_input)
    )
    dy_near = lax.all_gather(exchanged(early_dy), "expert", axis=0)
    mats = (own_gu, over_x(early_gu), own_down, over_x(early_down))
    positions = jnp.arange(tok_rows)
    live_rows = positions < lengths[0]
    valid_rows = live_rows.astype(jnp.float32)[:, None]
    input_full = full_input.astype(jnp.float32)
    scale_x = lax.rsqrt(jnp.mean(input_full * input_full, axis=-1, keepdims=True) + EPS)
    normed = (input_full * scale_x * g_attn).astype(jnp.bfloat16)
    q_raw = jnp.dot(normed, w_query, preferred_element_type=jnp.float32)
    k_raw = jnp.dot(normed, w_key, preferred_element_type=jnp.float32)
    values = jnp.dot(normed, w_value, preferred_element_type=jnp.float32).astype(jnp.bfloat16)
    q_total, k_total = tensor_sum(
        jnp.stack([jnp.sum(q_raw * q_raw, axis=1), jnp.sum(k_raw * k_raw, axis=1)])
    )
    scale_q = lax.rsqrt(q_total / model_width + EPS)[:, None]
    scale_k = lax.rsqrt(k_total / model_width + EPS)[:, None]
    q_norm = q_raw * scale_q * g_query
    k_norm = k_raw * scale_k * g_key
    cosine, sine_table = rotary_tables(SLOT, HD)
    head_shape = (SLOT, heads_here, HD)
    flat_shape = (tok_rows, heads_here * HD)
    query = rotate(q_norm.reshape(head_shape), cosine, sine_table).astype(bf16).reshape(flat_shape)
    keys = rotate(k_norm.reshape(head_shape), cosine, sine_table).astype(bf16).reshape(flat_shape)
    (heads_out,) = per_head(attend_body, lengths, (query, keys, values), [bf16], [])
    attn_slice = column_parts(
        lambda at: jnp.dot(
            heads_out,
            lax.dynamic_slice_in_dim(w_out, at, slice_width, 1),
            preferred_element_type=f32,
        ),
    )
    hidden = block_input.astype(f32) + attn_slice
    g_moe_slice = own_columns(g_moe)
    moe_rows = (hidden * g_moe_slice).astype(jnp.bfloat16)
    moe_piece = exchanged(moe_rows)
    moe_piece, dy_near = lax.optimization_barrier((moe_piece, dy_near))
    x_near = [
        lax.all_gather(v, "expert", axis=0) for v in jnp.split(moe_piece, n_steps, axis=1)
    ]
    router_slice = lax.dynamic_slice_in_dim(w_router, offset, slice_width, 0)
    statistics = jnp.concatenate(
        [
            jnp.dot(moe_rows, router_slice, preferred_element_type=jnp.float32),
            jnp.sum(hidden * hidden, axis=1, keepdims=True),
        ],
        axis=1,
    )
    statistics = tensor_sum(statistics.T).T
    scale_h = lax.rsqrt(statistics[:, n_experts:] / model_width + EPS)
    router_probs = jax.nn.softmax(statistics[:, :n_experts] * scale_h, axis=-1)
    expert_ids = jnp.arange(n_experts, dtype=jnp.int32)
    chosen = jnp.any(routes[:, :, None] == expert_ids[None, None, :], axis=1) & live_rows[:, None]
    chosen = chosen.astype(jnp.float32)
    gates = router_probs * chosen
    flat = jnp.concatenate(
        [
            gates.T,
            scale_h.T,
            jnp.full((1, tok_rows), lengths[0].astype(f32)),
            jnp.zeros((6, tok_rows), f32),
        ],
        axis=0,
    )
    flat = lax.all_gather(flat, "expert", axis=0)
    x_near[0], flat = lax.optimization_barrier((x_near[0], flat))
    all_lengths = flat[:, n_experts + 1, 0].astype(jnp.int32)
    info = jnp.concatenate(
        [
            lax.dynamic_slice_in_dim(flat, e_index * n_local, n_local, 1),
            flat[:, n_experts : n_experts + 1],
            jnp.zeros((n_expert, 8 - n_local - 1, tok_rows), f32),
        ],
        axis=1,
    )
    info = lax.dynamic_index_in_dim(info.reshape(n_expert, 8, -1, 2, stripe), x_index, 3, False)
    info = info.reshape(n_expert, 8, n_steps, -1).transpose(2, 0, 3, 1)
    part_rows = half // n_steps

    dy_pair = (dy_near, over_core(dy_near))
    out_parts, back_parts, extras, stacks = [], [], [], ()
    for step in range(n_steps):
        first = step * 2 * part_rows + x_index * stripe
        meta = jnp.concatenate([jnp.stack([t_index, first]), all_lengths])
        x_pair = (x_near[step], over_core(x_near[step]))
        outs, backs, stacks, dgate = act_call(
            step, n_steps, meta, x_pair, dy_pair, info[step], mats, n_local, stacks
        )
        out_parts.append(outs)
        rows = lax.dynamic_update_slice_in_dim(
            jnp.zeros((n_expert, n_experts, slice_width), f32),
            jnp.pad(
                dgate[:, :, :n_local].transpose(0, 2, 1),
                ((0, 0), (0, 0), (0, slice_width - part_rows)),
            ),
            e_index * n_local,
            1,
        )
        high = lax.reduce_precision(rows, 8, 7)
        extra = jnp.stack([high, rows - high], axis=1).astype(bf16)
        total = reduced(jnp.concatenate([joined(backs), extra], axis=2))
        back_parts.append(total[:, :part_rows])
        extra = total[:, part_rows:, :part_rows].astype(f32)
        extras.append(extra[0] + extra[1])
    x_stack, g_stack, pre_own, pre_other, inner_own, inner_other = [
        v.reshape(-1, v.shape[3]) for v in stacks
    ]
    other_down = over_x(cross_dot(inner_other, g_stack).astype(bf16))
    other_gu = cross_dot(x_stack, pre_other).astype(bf16)
    mine_gu = cross_dot(x_stack, pre_own)
    mine_down = cross_dot(inner_own, g_stack)
    out_message = jnp.concatenate([joined(parts) for parts in out_parts], axis=2)
    back_total = jnp.concatenate(back_parts, axis=1)
    back_total, out_message, other_gu, mine_gu, mine_down = lax.optimization_barrier(
        (back_total, out_message, other_gu, mine_gu, mine_down)
    )
    back_slice = home(back_total)
    moe_total = reduced(out_message)

    total = jnp.concatenate(extras, axis=1)
    total = total + over_core(total)
    d_gates = unstriped(total.T, over_x(total).T)

    d_probs = d_gates * chosen
    d_logits = (
        router_probs * (d_probs - jnp.sum(router_probs * d_probs, axis=-1, keepdims=True))
    ).astype(jnp.bfloat16)
    scaled_logits = (d_logits.astype(jnp.float32) * scale_h).astype(jnp.bfloat16)
    router_grad = cross_dot(moe_rows, scaled_logits)
    back_slice = back_slice + dot_transposed(scaled_logits, router_slice)
    projection = jnp.sum(back_slice * (hidden * g_moe_slice), axis=1)
    h_term = (tensor_sum(projection[None])[0] / model_width)[:, None] * scale_h * scale_h
    d_out_slice = cotangent.astype(f32) * valid_rows
    d_hidden_slice = d_out_slice + g_moe_slice * back_slice - hidden * h_term
    grad_g_moe = jnp.sum(back_slice * hidden, axis=0)
    d_attn = d_hidden_slice.astype(bf16)
    across = over_x(d_attn)
    d_attn = [d_attn, over_core(d_attn), across, over_core(across)]
    grad_w_out = jnp.concatenate([cross_dot(heads_out, v) for v in d_attn], axis=1)
    d_heads = sum(
        dot_transposed(
            v, lax.dynamic_slice_in_dim(w_out, (t_index ^ p) * slice_width, slice_width, 1)
        )
        for p, v in enumerate(d_attn)
    )
    d_heads = d_heads.astype(bf16)
    other_gu = over_x(other_gu)
    d_query, d_keys, d_values = per_head(
        attend_back_body,
        lengths,
        (query, keys, values, d_heads),
        [f32, f32, bf16],
        [pltpu.VMEM((tok_rows, HD), f32)],
    )
    d_q_norm = unrotate(d_query.reshape(head_shape), cosine, sine_table).reshape(tok_rows, heads_here * HD)
    d_k_norm = unrotate(d_keys.reshape(head_shape), cosine, sine_table).reshape(tok_rows, heads_here * HD)
    q_sum, k_sum = tensor_sum(
        jnp.stack(
            [jnp.sum(d_q_norm * g_query * q_raw, axis=1), jnp.sum(d_k_norm * g_key * k_raw, axis=1)]
        )
    )
    grad_g_query = jnp.sum(d_q_norm * q_raw * scale_q, axis=0)
    grad_g_key = jnp.sum(d_k_norm * k_raw * scale_k, axis=0)
    d_q_raw = (
        scale_q * g_query * d_q_norm - q_raw * scale_q**3 * (q_sum / model_width)[:, None]
    ).astype(jnp.bfloat16)
    d_k_raw = (
        scale_k * g_key * d_k_norm - k_raw * scale_k**3 * (k_sum / model_width)[:, None]
    ).astype(jnp.bfloat16)
    grad_w_query = cross_dot(normed, d_q_raw)
    grad_w_key = cross_dot(normed, d_k_raw)
    grad_w_value = cross_dot(normed, d_values)

    def normed_columns(at):
        def back(gradient, weight):
            return dot_transposed(gradient, lax.dynamic_slice_in_dim(weight, at, slice_width, 0))

        return back(d_q_raw, w_query) + back(d_k_raw, w_key) + back(d_values, w_value)

    column_sums = jnp.sum(
        d_q_raw.astype(jnp.float32) * q_raw
        + d_k_raw.astype(jnp.float32) * k_raw
        + d_values.astype(jnp.float32) * values.astype(jnp.float32),
        axis=1,
    )
    x_mean = (tensor_sum(column_sums[None])[0] / model_width)[:, None]
    d_normed = column_parts(normed_columns)
    x_hat = block_input.astype(jnp.float32) * scale_x
    grad_g_attn = jnp.sum(d_normed * x_hat, axis=0)
    grad_input = (
        d_hidden_slice + scale_x * (d_normed * own_columns(g_attn) - x_hat * x_mean)
    ).astype(jnp.bfloat16)

    sum_query, sum_key, sum_value = map(expert_sum, (grad_w_query, grad_w_key, grad_w_value))
    sum_out = lax.psum(grad_w_out.astype(bf16), "expert")
    sum_out = sum_out.astype(f32)
    moe_slice = home(moe_total)
    output = (valid_rows * (hidden + moe_slice)).astype(bf16)
    sum_out = jnp.concatenate(
        [
            lax.dynamic_slice_in_dim(sum_out, (t_index ^ p) * slice_width, slice_width, 1)
            for p in range(4)
        ],
        axis=1,
    )
    other_gu, other_down, _ = lax.optimization_barrier((other_gu, other_down, d_k_raw))
    grad_gu = mine_gu + other_gu.astype(f32)
    grad_w_down = (mine_down + other_down.astype(f32)).reshape(w_down.shape)
    grad_gu = grad_gu.reshape(model_width, 2, n_local, -1)
    grad_w_gate = grad_gu[:, 0].transpose(1, 0, 2)
    grad_w_up = grad_gu[:, 1].transpose(1, 0, 2)
    small = jnp.concatenate(
        [router_grad.T, grad_g_moe[None], grad_g_attn[None], grad_g_query[None], grad_g_key[None]],
        axis=0,
    )
    hop = 1
    while hop < n_expert:
        small = small + lax.ppermute(small, "expert", [(i, i ^ hop) for i in range(n_expert)])
        hop *= 2
    shared = tensor_sum(
        lax.dynamic_update_slice_in_dim(
            jnp.zeros((n_experts + 2, model_width), f32), small[: n_experts + 2], offset, 1
        )
    )
    return (
        output,
        grad_input,
        shared[n_experts + 1],
        sum_query,
        sum_key,
        sum_value,
        small[n_experts + 2],
        small[n_experts + 3],
        sum_out,
        shared[n_experts],
        shared[:n_experts].T,
        grad_w_gate,
        grad_w_up,
        grad_w_down,
    )


def solution(mesh):
    placed = (
        P("expert", "tensor"),
        P("expert", "tensor"),
        P("expert"),
        P("expert", None),
        P(),
        P(None, "tensor"),
        P(None, "tensor"),
        P(None, "tensor"),
        P("tensor"),
        P("tensor"),
        P("tensor", None),
        P(),
        P(),
        P("expert", None, "tensor"),
        P("expert", None, "tensor"),
        P("expert", "tensor", None),
    )
    return jax.shard_map(
        layer,
        mesh=mesh,
        in_specs=placed,
        out_specs=(
            P("expert", "tensor"),
            P("expert", "tensor"),
            P(),
            P(None, "tensor"),
            P(None, "tensor"),
            P(None, "tensor"),
            P("tensor"),
            P("tensor"),
            P("tensor", None),
            P(),
            P(),
            P("expert", None, "tensor"),
            P("expert", None, "tensor"),
            P("expert", "tensor", None),
        ),
        check_vma=False,
    )
```
